32 devices in a mesh: groups: 2 (over y), frame: 8 (over z, x), head: 2 (over core).
Axes of the slice: x: 2, y: 2, z: 4, core: 2. Of those that a mesh axis runs over, the one named last changes fastest.
Arguments:
- head_queries: bfloat16 [4096, 1536], P(('groups', 'frame'), 'head'), parts along dimension 0, may hold values from -10 to 10
- head_keys: bfloat16 [4096, 1536], P(('groups', 'frame'), 'head'), parts along dimension 0, may hold values from -10 to 10
- head_values: bfloat16 [4096, 1536], P(('groups', 'frame'), 'head'), parts along dimension 0, may hold values from -18 to 18
- out_weight: bfloat16 [1536, 3072], P('head', 'frame'), may hold values from -0.15625 to 0.15625
- head_class: int32 [12], P('head'), may hold values from 0 to 1, as said below
- block_lists: int32 [12, 16, 4, 2], P('head', ('groups', 'frame')), parts along dimension 1, may hold values from 0 to 3, as said below
- block_counts: int32 [12, 16, 4], P('head', ('groups', 'frame')), parts along dimension 1, may hold values from 1 to 2, as said below
Outputs:
- projected: bfloat16 [4096, 3072], P(('groups', 'frame', 'head')), parts along dimension 0
The draws below stay inside these ranges and needn't reach their ends.
There are 2 independent parts, one for each index of `groups`. The reference program is written for one: setup_inputs(seed, part) draws one part's arguments, and reference() takes and returns one part's arrays. A program takes and returns all parts, laid end to end along the dimension named above; an argument that names none is the same for every part. Nothing has to cross between parts.
Inputs may be any that keep to these rules, and one draw needn't show every extreme that they name: `head_class`: for each j from 0 to 1, exactly half of the heads j * 6 to (j + 1) * 6 - 1 are temporal. block_lists[h, g, b, 0] equals b, and the entries of one list are distinct. `block_counts`: for each head and sequence some query block uses all 2 entries.
All inputs are finite; a program needn't handle non-finite values.
Results may differ from the reference program's by a relative error of at most 0.0062.
Values may be sent and summed in bfloat16 or wider, within the bound.
No kernel may reach another device: no remote copies, remote signals or barrier semaphores. Data moves between devices by JAX's collectives and lax.ppermute only.
A program may use at most 64 MiB of HBM per device.

```python
import jax
import jax.numpy as jnp
from jax import lax

D = 3072
HEADS = 12
HEAD_DIM = 128
PIX = 256
FRAMES = 8
TOKENS = 2048
PXD = 32
NB = 4
KMAX = 2
N_FRAME = 8
N_HEAD = 2


def query_key_pair(key):
    dims_all = (TOKENS, HEADS * HEAD_DIM)
    key_a, key_b = jax.random.split(jax.random.fold_in(key, 11))
    queries_f = jnp.clip(1.2 * jax.random.normal(key_a, dims_all, jnp.float32), -4.8, 4.8)
    keys_f = jnp.clip(1.2 * jax.random.normal(key_b, dims_all, jnp.float32), -4.8, 4.8)
    return (queries_f, keys_f)


def draw_head_queries(key, part):
    return query_key_pair(key)[0].astype(jnp.bfloat16)


def draw_head_keys(key, part):
    return query_key_pair(key)[1].astype(jnp.bfloat16)


def draw_head_class(key, part):
    per_shard = HEADS // N_HEAD
    shard_keys = jax.random.split(jax.random.fold_in(key, 5), N_HEAD)
    ranking = jax.vmap(lambda single: jax.random.permutation(single, per_shard))(shard_keys)
    return (ranking < per_shard // 2).astype(jnp.int32).reshape(HEADS)


def draw_block_lists(key, part):
    total_rows = HEADS * N_FRAME * NB
    row_keys = jax.random.split(jax.random.fold_in(key, 21), total_rows)
    others = jax.vmap(lambda single: jax.random.permutation(single, NB - 1))(row_keys).astype(jnp.int32)
    own_block = (jnp.arange(total_rows, dtype=jnp.int32) % NB)[:, None]
    others = others + (others >= own_block).astype(jnp.int32)
    listed = jnp.concatenate([own_block, others[:, :KMAX - 1]], axis=1)
    return listed.reshape(HEADS, N_FRAME, NB, KMAX).astype(jnp.int32)


def draw_block_counts(key, part):
    key_a, key_b, key_c = jax.random.split(jax.random.fold_in(key, 31), 3)
    levels = jax.random.randint(key_a, (1, N_FRAME, 1), 1, KMAX + 1)
    counts = jax.random.randint(key_b, (HEADS, N_FRAME, NB), 1, levels + 1)
    full_spot = jax.random.randint(key_c, (HEADS, N_FRAME, 1), 0, NB)
    counts = jnp.where(jnp.arange(NB)[None, None, :] == full_spot, KMAX, counts)
    return counts.astype(jnp.int32)


def block_scale(key, dims, cuts, least, top_value):
    def one(dim, blocks):
        steps = jax.random.uniform(jax.random.fold_in(jax.random.fold_in(key, 6), dim), (blocks,), jnp.float32, least / len(cuts), top_value / len(cuts))
        return jnp.repeat(jnp.exp(steps), dims[dim] // blocks).reshape((-1,) + (1,) * (len(dims) - dim - 1))

    gain = one(*cuts[0])
    for cut in cuts[1:]:
        gain = gain * one(*cut)
    return gain


def scatter_about(own_key, shape, spread, reach, cuts=(), kind=jnp.bfloat16):
    entries = jax.random.normal(own_key, shape, jnp.float32) * spread
    if len(cuts) > 0:
        entries = block_scale(own_key, shape, cuts, -0.22, 0.18) * entries
    return jnp.clip(entries, min=-reach, max=reach).astype(kind)


def setup_inputs(seed: int = 0, part: int = 0) -> dict:
    key_of = jax.random.split(jax.random.key(seed), 8)
    part_keys = jax.random.split(jax.random.fold_in(key_of[7], part), 8)
    head_queries = draw_head_queries(jax.random.fold_in(jax.random.fold_in(key_of[7], part), 71), part)
    head_keys = draw_head_keys(jax.random.fold_in(jax.random.fold_in(key_of[7], part), 71), part)
    head_values = scatter_about(part_keys[2], (TOKENS, HEADS * HEAD_DIM), 3.0, 18.0, ((0, 8), (1, 2)))
    out_weight = scatter_about(key_of[3], (HEADS * HEAD_DIM, D), (HEADS * HEAD_DIM) ** -0.5, 0.15625, ((0, 2), (1, 8)))
    head_class = draw_head_class(jax.random.fold_in(key_of[7], 71), part)
    block_lists = draw_block_lists(jax.random.fold_in(jax.random.fold_in(key_of[7], part), 71), part)
    block_counts = draw_block_counts(jax.random.fold_in(jax.random.fold_in(key_of[7], part), 71), part)
    return {"head_queries": head_queries, "head_keys": head_keys, "head_values": head_values, "out_weight": out_weight, "head_class": head_class, "block_lists": block_lists, "block_counts": block_counts}


def attend_group(queries_h, keys_h, values_h, block_ids, counts):
    block_count = block_ids.shape[0]
    listed_most = block_ids.shape[1]
    block_rows = queries_h.shape[0] // block_count
    usable = jnp.arange(listed_most)[None, :] < counts[:, None]
    linked = jnp.any(usable[:, :, None] & (block_ids[:, :, None] == jnp.arange(block_count)[None, None, :]), axis=1)
    allowed = jnp.repeat(jnp.repeat(linked, block_rows, axis=0), block_rows, axis=1)
    scores = jnp.dot(queries_h, keys_h.T, preferred_element_type=jnp.float32) * (HEAD_DIM ** -0.5)
    scores = jnp.where(allowed, scores, -jnp.inf)
    row_max = jnp.max(scores, axis=1, keepdims=True)
    weights = jnp.exp(scores - row_max)
    denominator = jnp.sum(weights, axis=1, keepdims=True)
    rounded = weights.astype(jnp.bfloat16)
    result = jnp.dot(rounded, values_h, preferred_element_type=jnp.float32) / denominator
    return result.astype(jnp.bfloat16)


def reference(head_queries, head_keys, head_values, out_weight, head_class, block_lists, block_counts):
    position = jnp.arange(TOKENS, dtype=jnp.int32)
    group_of = position // PIX
    within = position % PIX
    layout_in_t = (within // PXD) * PIX + group_of * PXD + within % PXD
    frame_of = position // PIX
    pixel_of = position % PIX
    layout_out_t = (pixel_of // PXD) * PIX + frame_of * PXD + pixel_of % PXD

    def heads_first(tensor):
        return tensor.reshape(TOKENS, HEADS, HEAD_DIM).transpose(1, 0, 2)

    def one_head(inputs):
        queries_h, keys_h, values_h, head_kind, block_ids, counts = inputs
        layout_in = jnp.where(head_kind == 1, layout_in_t, position)
        layout_out = jnp.where(head_kind == 1, layout_out_t, position)
        grouped_q = jnp.take(queries_h, layout_in, axis=0).reshape(FRAMES, PIX, HEAD_DIM)
        grouped_k = jnp.take(keys_h, layout_in, axis=0).reshape(FRAMES, PIX, HEAD_DIM)
        grouped_v = jnp.take(values_h, layout_in, axis=0).reshape(FRAMES, PIX, HEAD_DIM)
        result = jax.vmap(attend_group)(grouped_q, grouped_k, grouped_v, block_ids, counts)
        return jnp.take(result.reshape(TOKENS, HEAD_DIM), layout_out, axis=0)

    attended = lax.map(one_head, (heads_first(head_queries), heads_first(head_keys), heads_first(head_values), head_class, block_lists, block_counts))
    attended = attended.transpose(1, 0, 2).reshape(TOKENS, HEADS * HEAD_DIM)
    stride = (HEADS // N_HEAD) * HEAD_DIM

    def project_rows(row_block):
        summed = jnp.zeros((row_block.shape[0], D), jnp.float32)
        for member in range(N_HEAD):
            portion = jnp.dot(row_block[:, member * stride:(member + 1) * stride], out_weight[member * stride:(member + 1) * stride], preferred_element_type=jnp.float32).astype(jnp.bfloat16)
            summed = summed + lax.optimization_barrier(portion).astype(jnp.float32)
        return summed.astype(jnp.bfloat16)

    projected = lax.map(project_rows, attended.reshape(FRAMES, PIX, HEADS * HEAD_DIM))
    return projected.reshape(TOKENS, D)
```

```python
import functools

import jax
import jax.numpy as jnp
from jax import lax
from jax.experimental import pallas as pl
from jax.experimental.pallas import tpu as pltpu
from jax.sharding import PartitionSpec as P

VMEM = pl.BlockSpec(memory_space=pltpu.VMEM)
SMEM = pl.BlockSpec(memory_space=pltpu.SMEM)
PARAMS = pltpu.CompilerParams(vmem_limit_bytes=40 * 1024 * 1024)


def head_of_rank(class_ref, kind, rank, heads):
    found = jnp.int32(0)
    seen = jnp.int32(0)
    for head in range(heads):
        is_kind = class_ref[head] == kind
        found = jnp.where(is_kind & (seen == rank), head, found)
        seen = seen + is_kind.astype(jnp.int32)
    return found


def columns(index, width):
    return pl.ds(pl.multiple_of(index * width, width), width)


def pack_kernel(heads, width, class_ref, q_ref, k_ref, v_ref, packed_ref):
    half = heads // 2
    for rank in range(half):
        head = head_of_rank(class_ref, 1, rank, heads)
        for place, ref in enumerate((q_ref, k_ref, v_ref)):
            at = (place * half + rank) * width
            packed_ref[:, at : at + width] = ref[:, columns(head, width)]


def attend(queries, keys, values, listed, blocks):
    rows = queries.shape[0] // blocks
    scores = lax.dot_general(
        queries, keys, (((1,), (1,)), ((), ())), preferred_element_type=jnp.float32
    ) * (queries.shape[1] ** -0.5)
    key_block = lax.broadcasted_iota(jnp.int32, (rows, keys.shape[0]), 1) // rows
    masked = []
    for block in range(blocks):
        first, second = listed[block]
        allowed = (key_block == first) | (key_block == second)
        masked.append(
            jnp.where(allowed, scores[block * rows : (block + 1) * rows], -jnp.inf)
        )
    scores = jnp.concatenate(masked, axis=0)
    weights = jnp.exp(scores - jnp.max(scores, axis=1, keepdims=True))
    denominator = jnp.sum(weights, axis=1, keepdims=True)
    total = jnp.dot(
        weights.astype(jnp.bfloat16), values, preferred_element_type=jnp.float32
    )
    return (total / denominator).astype(jnp.bfloat16)


def listed_blocks(lists_ref, counts_ref, head, blocks):
    listed = []
    for block in range(blocks):
        first = lists_ref[head * 2 * blocks + 2 * block]
        second = lists_ref[head * 2 * blocks + 2 * block + 1]
        listed.append(
            (first, jnp.where(counts_ref[head * blocks + block] > 1, second, first))
        )
    return listed


def spatial_kernel(
    heads, width, blocks, class_ref, lists_ref, counts_ref, q_ref, k_ref, v_ref, out_ref
):
    for rank in range(heads // 2):
        head = head_of_rank(class_ref, 0, rank, heads)
        at = columns(head, width)
        out_ref[:, rank * width : (rank + 1) * width] = attend(
            q_ref[:, at],
            k_ref[:, at],
            v_ref[:, at],
            listed_blocks(lists_ref, counts_ref, head, blocks),
            blocks,
        )


def temporal_kernel(
    heads, width, blocks, class_ref, lists_ref, counts_ref, packed_ref, out_ref
):
    half = heads // 2
    for rank in range(half):
        head = head_of_rank(class_ref, 1, rank, heads)
        q, k, v = (
            packed_ref[:, (place * half + rank) * width : (place * half + rank + 1) * width]
            for place in range(3)
        )
        out_ref[:, rank * width : (rank + 1) * width] = attend(
            q, k, v, listed_blocks(lists_ref, counts_ref, head, blocks), blocks
        )


def place_heads(heads, width, class_ref, spatial_ref, temporal_ref, att_ref):
    for kind, ref in ((0, spatial_ref), (1, temporal_ref)):
        for rank in range(heads // 2):
            head = head_of_rank(class_ref, kind, rank, heads)
            att_ref[:, columns(head, width)] = ref[:, rank * width : (rank + 1) * width]


def project_pieces_kernel(
    heads, width, count, class_ref, at_ref, spatial_ref, temporal_ref, *refs
):
    pieces, (peer_ref, mine_ref, att_ref) = refs[: 2 * count], refs[2 * count :]
    place_heads(heads, width, class_ref, spatial_ref, temporal_ref, att_ref)
    depth, cols = pieces[0].shape
    rows = peer_ref.shape[0]
    half = at_ref[count]
    side = at_ref[count + 1]
    for out_ref, part in ((peer_ref, 1 - side), (mine_ref, side)):
        take = pl.ds(pl.multiple_of(part * rows, rows), rows)
        left = att_ref[take, columns(half, depth)]
        right = att_ref[take, columns(1 - half, depth)]
        for index in range(count):
            total = jnp.dot(
                left, pieces[2 * index][...], preferred_element_type=jnp.float32
            ) + jnp.dot(
                right, pieces[2 * index + 1][...], preferred_element_type=jnp.float32
            )
            out_ref[:, columns(at_ref[index], cols)] = total.astype(out_ref.dtype)


def project_whole_kernel(
    heads, width, class_ref, at_ref, spatial_ref, temporal_ref, weight_ref, peer_ref, mine_ref, att_ref
):
    place_heads(heads, width, class_ref, spatial_ref, temporal_ref, att_ref)
    rows = peer_ref.shape[0]
    side = at_ref[0]
    for out_ref, part in ((peer_ref, 1 - side), (mine_ref, side)):
        take = pl.ds(pl.multiple_of(part * rows, rows), rows)
        out_ref[...] = jnp.dot(
            att_ref[take, :], weight_ref[...], preferred_element_type=jnp.float32
        ).astype(out_ref.dtype)


def gather_pieces(shard):
    rows = shard.shape[0] // 2
    group = lax.axis_index("groups")
    index = lax.axis_index("frame")
    line, pair = index // 2, index % 2

    def swap_pair(piece):
        return lax.ppermute(piece, "frame", [(i, i ^ 1) for i in range(8)])

    def swap_group(piece):
        return lax.ppermute(piece, "groups", [(0, 1), (1, 0)])

    def next_line(piece):
        return lax.ppermute(piece, "frame", [(i, (i + 2) % 8) for i in range(8)])

    mine = lax.dynamic_slice_in_dim(shard, group * rows, rows, 0)
    other = lax.dynamic_slice_in_dim(shard, (1 - group) * rows, rows, 0)
    across = swap_pair(shard)
    pieces = [
        (mine, other, index),
        (
            lax.dynamic_slice_in_dim(across, group * rows, rows, 0),
            lax.dynamic_slice_in_dim(across, (1 - group) * rows, rows, 0),
            index ^ 1,
        ),
    ]
    held = mine
    for step in (1, 2, 3):
        held = next_line(held)
        source = ((line - step) % 4) * 2
        held_pair = swap_pair(held)
        held_group = swap_group(held)
        last = swap_pair(held_group) if step == 3 else swap_group(held_pair)
        pieces.append((held, held_group, source + pair))
        pieces.append((held_pair, last, source + 1 - pair))
    return pieces


def on_device(
    head_queries, head_keys, head_values, out_weight, head_class, block_lists, block_counts
):
    pixels = head_queries.shape[0]
    heads = head_class.shape[0]
    half = heads // 2
    width = head_queries.shape[1] // heads
    blocks = block_counts.shape[2]
    frames = lax.axis_size("frame")
    groups = lax.axis_size("groups")
    model = out_weight.shape[1] * frames
    side = lax.axis_index("head")
    bf16 = functools.partial(jax.ShapeDtypeStruct, dtype=jnp.bfloat16)
    lists = block_lists.reshape(-1)
    counts = block_counts.reshape(-1)

    packed = pl.pallas_call(
        functools.partial(pack_kernel, heads, width),
        out_shape=bf16((pixels, 3 * half * width)),
        in_specs=[SMEM, VMEM, VMEM, VMEM],
        out_specs=VMEM,
        compiler_params=PARAMS,
    )(head_class, head_queries, head_keys, head_values)
    arrived = lax.all_to_all(
        packed.reshape(frames, pixels // frames, 3 * half * width),
        "frame",
        split_axis=0,
        concat_axis=0,
        tiled=True,
    ).reshape(pixels, 3 * half * width)
    spatial = pl.pallas_call(
        functools.partial(spatial_kernel, heads, width, blocks),
        out_shape=bf16((pixels, half * width)),
        in_specs=[SMEM, SMEM, SMEM, VMEM, VMEM, VMEM],
        out_specs=VMEM,
        compiler_params=PARAMS,
    )(head_class, lists, counts, head_queries, head_keys, head_values)
    temporal = pl.pallas_call(
        functools.partial(temporal_kernel, heads, width, blocks),
        out_shape=bf16((pixels, half * width)),
        in_specs=[SMEM, SMEM, SMEM, VMEM],
        out_specs=VMEM,
        compiler_params=PARAMS,
    )(head_class, lists, counts, arrived)
    returned = lax.all_to_all(
        temporal.reshape(frames, pixels // frames, half * width),
        "frame",
        split_axis=0,
        concat_axis=0,
        tiled=True,
    ).reshape(pixels, half * width)

    portion_shapes = [bf16((pixels // 2, model))] * 2
    scratch = [pltpu.VMEM((pixels, heads * width), jnp.bfloat16)]
    if frames == 8 and groups == 2:
        pieces = gather_pieces(out_weight)
        at = jnp.stack(
            [piece[2] for piece in pieces] + [lax.axis_index("groups"), side]
        ).astype(jnp.int32)
        operands = [ref for piece in pieces for ref in piece[:2]]
        peer, mine = pl.pallas_call(
            functools.partial(project_pieces_kernel, heads, width, len(pieces)),
            out_shape=portion_shapes,
            in_specs=[SMEM, SMEM] + [VMEM] * (2 + len(operands)),
            out_specs=[VMEM, VMEM],
            scratch_shapes=scratch,
            compiler_params=PARAMS,
        )(head_class, at, spatial, returned, *operands)
    else:
        weight = lax.all_gather(out_weight, "frame", axis=1, tiled=True)
        peer, mine = pl.pallas_call(
            functools.partial(project_whole_kernel, heads, width),
            out_shape=portion_shapes,
            in_specs=[SMEM, SMEM] + [VMEM] * 3,
            out_specs=[VMEM, VMEM],
            scratch_shapes=scratch,
            compiler_params=PARAMS,
        )(head_class, side.reshape(1).astype(jnp.int32), spatial, returned, weight)
    received = lax.ppermute(peer, "head", [(0, 1), (1, 0)])
    return (mine.astype(jnp.float32) + received.astype(jnp.float32)).astype(jnp.bfloat16)


def solution(mesh):
    placed = (
        P(("groups", "frame"), "head"),
        P(("groups", "frame"), "head"),
        P(("groups", "frame"), "head"),
        P("head", "frame"),
        P("head"),
        P("head", ("groups", "frame"), None, None),
        P("head", ("groups", "frame"), None),
    )
    return jax.shard_map(
        on_device,
        mesh=mesh,
        in_specs=placed,
        out_specs=P(("groups", "frame", "head"), None),
        check_vma=False,
    )
```

```python
import functools

import jax
import jax.numpy as jnp
from jax import lax
from jax.experimental import pallas as pl
from jax.experimental.pallas import tpu as pltpu
from jax.sharding import PartitionSpec as P

VMEM = pl.BlockSpec(memory_space=pltpu.VMEM)
SMEM = pl.BlockSpec(memory_space=pltpu.SMEM)
ANY = pl.BlockSpec(memory_space=pl.ANY)
PARAMS = pltpu.CompilerParams(vmem_limit_bytes=40 * 1024 * 1024)


def head_of_rank(class_ref, kind, rank, heads):
    found = jnp.int32(0)
    seen = jnp.int32(0)
    for head in range(heads):
        is_kind = class_ref[head] == kind
        found = jnp.where(is_kind & (seen == rank), head, found)
        seen = seen + is_kind.astype(jnp.int32)
    return found


def columns(index, width):
    return pl.ds(pl.multiple_of(index * width, width), width)


def head_copies(heads, width, kind, class_ref, sources, place, sems):
    copies = []
    for rank in range(heads // 2):
        head = head_of_rank(class_ref, kind, rank, heads)
        for index, source in enumerate(sources):
            copies.append(
                pltpu.make_async_copy(
                    source.at[:, columns(head, width)],
                    place(index, rank),
                    sems.at[index, rank],
                )
            )
    for copy in copies:
        copy.start()
    return copies


def pack_kernel(heads, width, class_ref, q_ref, k_ref, v_ref, packed_ref, sems):
    def place(index, rank):
        at = (index * (heads // 2) + rank) * width
        return packed_ref.at[:, at : at + width]

    for copy in head_copies(heads, width, 1, class_ref, (q_ref, k_ref, v_ref), place, sems):
        copy.wait()


def attend(queries, keys, values, listed, blocks):
    rows = queries.shape[0] // blocks
    scores = lax.dot_general(
        queries, keys, (((1,), (1,)), ((), ())), preferred_element_type=jnp.float32
    ) * (queries.shape[1] ** -0.5)
    key_block = lax.broadcasted_iota(jnp.int32, (rows, keys.shape[0]), 1) // rows
    masked = []
    for block in range(blocks):
        first, second = listed[block]
        allowed = (key_block == first) | (key_block == second)
        masked.append(
            jnp.where(allowed, scores[block * rows : (block + 1) * rows], -jnp.inf)
        )
    scores = jnp.concatenate(masked, axis=0)
    weights = jnp.exp(scores - jnp.max(scores, axis=1, keepdims=True))
    denominator = jnp.sum(weights, axis=1, keepdims=True)
    total = jnp.dot(
        weights.astype(jnp.bfloat16), values, preferred_element_type=jnp.float32
    )
    return (total / denominator).astype(jnp.bfloat16)


def listed_blocks(lists_ref, head, blocks):
    listed = []
    for block in range(blocks):
        both = lists_ref[head * blocks + block]
        listed.append((both >> 8, both & 255))
    return listed


def spatial_kernel(
    heads, width, blocks, class_ref, lists_ref, q_ref, k_ref, v_ref, out_ref, held_ref, sems
):
    copies = head_copies(
        heads,
        width,
        0,
        class_ref,
        (q_ref, k_ref, v_ref),
        lambda index, rank: held_ref.at[index, rank],
        sems,
    )
    for rank in range(heads // 2):
        head = head_of_rank(class_ref, 0, rank, heads)
        for copy in copies[3 * rank : 3 * rank + 3]:
            copy.wait()
        out_ref[:, rank * width : (rank + 1) * width] = attend(
            held_ref[0, rank],
            held_ref[1, rank],
            held_ref[2, rank],
            listed_blocks(lists_ref, head, blocks),
            blocks,
        )


def temporal_kernel(
    heads, width, blocks, class_ref, lists_ref, packed_ref, out_ref
):
    half = heads // 2
    for rank in range(half):
        head = head_of_rank(class_ref, 1, rank, heads)
        q, k, v = (
            packed_ref[:, (place * half + rank) * width : (place * half + rank + 1) * width]
            for place in range(3)
        )
        out_ref[:, rank * width : (rank + 1) * width] = attend(
            q, k, v, listed_blocks(lists_ref, head, blocks), blocks
        )


def place_heads(heads, width, class_ref, spatial_ref, temporal_ref, att_ref):
    for kind, ref in ((0, spatial_ref), (1, temporal_ref)):
        for rank in range(heads // 2):
            head = head_of_rank(class_ref, kind, rank, heads)
            att_ref[:, columns(head, width)] = ref[:, rank * width : (rank + 1) * width]


def project_pieces_kernel(heads, width, count, class_ref, spatial_ref, temporal_ref, *refs):
    pieces, (peer_ref, mine_ref, att_ref, held_ref, sems) = refs[: 2 * count], refs[2 * count :]
    copies = [
        pltpu.make_async_copy(piece, held_ref.at[index], sems.at[index])
        for index, piece in enumerate(pieces)
    ]
    for copy in copies:
        copy.start()
    place_heads(heads, width, class_ref, spatial_ref, temporal_ref, att_ref)
    depth, cols = pieces[0].shape
    rows = peer_ref.shape[0]
    half = lax.axis_index("groups")
    side = lax.axis_index("head")
    for index in range(count):
        take = slice(index * cols, (index + 1) * cols)
        copies[2 * index].wait()
        total = jnp.dot(
            att_ref[:, columns(half, depth)],
            held_ref[2 * index],
            preferred_element_type=jnp.float32,
        )
        copies[2 * index + 1].wait()
        total += jnp.dot(
            att_ref[:, columns(1 - half, depth)],
            held_ref[2 * index + 1],
            preferred_element_type=jnp.float32,
        )
        total = total.astype(peer_ref.dtype)

        @pl.when(side == 0)
        def _():
            mine_ref[:, take] = total[:rows]
            peer_ref[:, take] = total[rows:]

        @pl.when(side != 0)
        def _():
            mine_ref[:, take] = total[rows:]
            peer_ref[:, take] = total[:rows]


def project_whole_kernel(
    heads, width, class_ref, spatial_ref, temporal_ref, weight_ref, peer_ref, mine_ref, att_ref
):
    place_heads(heads, width, class_ref, spatial_ref, temporal_ref, att_ref)
    rows = peer_ref.shape[0]
    side = lax.axis_index("head")
    for out_ref, part in ((peer_ref, 1 - side), (mine_ref, side)):
        take = pl.ds(pl.multiple_of(part * rows, rows), rows)
        out_ref[...] = jnp.dot(
            att_ref[take, :], weight_ref[...], preferred_element_type=jnp.float32
        ).astype(out_ref.dtype)


def join_kernel(shards, *refs):
    parts, out_ref = refs[:-1], refs[-1]
    index = lax.axis_index("frame")
    line, pair = index // 2, index % 2
    cols = out_ref.shape[1] // 8
    order = iter(shards)
    for mine_ref, received_ref in zip(parts[0::2], parts[1::2]):
        for at in range(mine_ref.shape[1] // cols):
            step, crossed = next(order)
            source = lax.rem(line - step + 4, 4) * 2 + (1 - pair if crossed else pair)
            take = slice(at * cols, (at + 1) * cols)
            total = mine_ref[:, take].astype(jnp.float32) + received_ref[:, take].astype(
                jnp.float32
            )
            out_ref[:, columns(source, cols)] = total.astype(out_ref.dtype)


def swap_pair(piece):
    return lax.ppermute(piece, "frame", [(i, i ^ 1) for i in range(8)])


def swap_group(piece):
    return lax.ppermute(piece, "groups", [(0, 1), (1, 0)])


def next_line(piece):
    return lax.ppermute(piece, "frame", [(i, (i + 2) % 8) for i in range(8)])


def swap_side(portion):
    return lax.ppermute(portion, "head", [(0, 1), (1, 0)])


def tied(*values):
    return lax.optimization_barrier(values)


def on_device(
    head_queries, head_keys, head_values, out_weight, head_class, block_lists, block_counts
):
    pixels = head_queries.shape[0]
    heads = head_class.shape[0]
    half = heads // 2
    width = head_queries.shape[1] // heads
    blocks = block_counts.shape[2]
    frames = lax.axis_size("frame")
    groups = lax.axis_size("groups")
    model = out_weight.shape[1] * frames
    bf16 = functools.partial(jax.ShapeDtypeStruct, dtype=jnp.bfloat16)
    first, second = block_lists[:, 0, :, 0], block_lists[:, 0, :, 1]
    lists = (first * 256 + jnp.where(block_counts[:, 0] > 1, second, first)).reshape(-1)

    def call(kernel, ins, outs, *operands, scratch=()):
        return pl.pallas_call(
            kernel,
            out_shape=outs,
            in_specs=ins,
            out_specs=jax.tree.map(lambda _: VMEM, outs),
            scratch_shapes=scratch,
            compiler_params=PARAMS,
            cost_estimate=pl.CostEstimate(flops=2000000000, bytes_accessed=8000000, transcendentals=0),
        )(*operands)

    def exchange(rows):
        split = rows.reshape(frames, pixels // frames, rows.shape[1])
        return lax.all_to_all(
            split, "frame", split_axis=0, concat_axis=0, tiled=True
        ).reshape(rows.shape)

    packed = call(
        functools.partial(pack_kernel, heads, width),
        [SMEM, ANY, ANY, ANY],
        bf16((pixels, 3 * half * width)),
        head_class,
        head_queries,
        head_keys,
        head_values,
        scratch=[pltpu.SemaphoreType.DMA((3, half))],
    )

    def spatial_heads():
        return call(
            functools.partial(spatial_kernel, heads, width, blocks),
            [SMEM, SMEM, ANY, ANY, ANY],
            bf16((pixels, half * width)),
            head_class,
            lists,
            head_queries,
            head_keys,
            head_values,
            scratch=[
                pltpu.VMEM((3, half, pixels, width), jnp.bfloat16),
                pltpu.SemaphoreType.DMA((3, half)),
            ],
        )

    def temporal_heads(arrived):
        return call(
            functools.partial(temporal_kernel, heads, width, blocks),
            [SMEM, SMEM, VMEM],
            bf16((pixels, half * width)),
            head_class,
            lists,
            arrived,
        )

    att_scratch = [pltpu.VMEM((pixels, heads * width), jnp.bfloat16)]
    if frames != 8 or groups != 2:
        spatial = spatial_heads()
        returned = exchange(temporal_heads(exchange(packed)))
        weight = lax.all_gather(out_weight, "frame", axis=1, tiled=True)
        peer, mine = call(
            functools.partial(project_whole_kernel, heads, width),
            [SMEM, VMEM, VMEM, VMEM],
            [bf16((pixels // 2, model))] * 2,
            head_class,
            spatial,
            returned,
            weight,
            scratch=att_scratch,
        )
        received = swap_side(peer)
        return (mine.astype(jnp.float32) + received.astype(jnp.float32)).astype(jnp.bfloat16)

    depth, cols = out_weight.shape[0] // 2, out_weight.shape[1]
    group = lax.axis_index("groups")
    own = lax.dynamic_slice_in_dim(out_weight, group * depth, depth, 0)
    rest = lax.dynamic_slice_in_dim(out_weight, (1 - group) * depth, depth, 0)

    def project(pieces):
        count = len(pieces) // 2
        return call(
            functools.partial(project_pieces_kernel, heads, width, count),
            [SMEM, VMEM, VMEM] + [ANY] * len(pieces),
            [bf16((pixels // 2, count * cols))] * 2,
            head_class,
            spatial,
            returned,
            *pieces,
            scratch=att_scratch
            + [
                pltpu.VMEM((len(pieces), depth, cols), jnp.bfloat16),
                pltpu.SemaphoreType.DMA((len(pieces),)),
            ],
        )

    arrived = exchange(packed)
    held_1, pair_0, spatial = tied(next_line(own), swap_pair(out_weight), spatial_heads())
    held_2, pair_1, rest_1, arrived = tied(
        next_line(held_1), swap_pair(held_1), swap_group(held_1), arrived
    )
    temporal, held_2, pair_1, rest_1 = tied(temporal_heads(arrived), held_2, pair_1, rest_1)
    returned = exchange(temporal)
    held_3, pair_2, pair_rest_1, rest_1 = tied(
        next_line(held_2), swap_pair(held_2), swap_group(pair_1), rest_1
    )
    rest_2, pair_3, rest_3, returned = tied(
        next_line(rest_1), swap_pair(held_3), swap_group(held_3), returned
    )
    pair_rest_2, pair_rest_3 = swap_group(pair_2), swap_pair(rest_3)
    across = [
        lax.dynamic_slice_in_dim(pair_0, start * depth, depth, 0) for start in (group, 1 - group)
    ]
    peer, mine = project(
        [own, rest, *across, held_1, rest_1, pair_1, pair_rest_1, held_2, rest_2, held_3, rest_3]
    )
    received = swap_side(peer)
    last_peer, last_mine = project([pair_2, pair_rest_2, pair_3, pair_rest_3])
    last_received = swap_side(last_peer)
    order = ((0, 0), (0, 1), (1, 0), (1, 1), (2, 0), (3, 0), (2, 1), (3, 1))
    return call(
        functools.partial(join_kernel, order),
        [VMEM] * 4,
        bf16((pixels // 2, model)),
        mine,
        received,
        last_mine,
        last_received,
    )


def solution(mesh):
    placed = (
        P(("groups", "frame"), "head"),
        P(("groups", "frame"), "head"),
        P(("groups", "frame"), "head"),
        P("head", "frame"),
        P("head"),
        P("head", ("groups", "frame"), None, None),
        P("head", ("groups", "frame"), None),
    )
    return jax.shard_map(
        on_device,
        mesh=mesh,
        in_specs=placed,
        out_specs=P(("groups", "frame", "head"), None),
        check_vma=False,
    )
```

```python
import functools

import jax
import jax.numpy as jnp
from jax import lax
from jax.experimental import pallas as pl
from jax.experimental.pallas import tpu as pltpu
from jax.sharding import PartitionSpec as P

VMEM = pl.BlockSpec(memory_space=pltpu.VMEM)
SMEM = pl.BlockSpec(memory_space=pltpu.SMEM)
ANY = pl.BlockSpec(memory_space=pl.ANY)
COSTS = {"pack": 1, "lists": 10000, "spatial": 2000, "temporal": 10000, "join": 10000, "add": 5000, "project": 20000}
PARAMS = pltpu.CompilerParams(vmem_limit_bytes=16 * 1024 * 1024)


def head_of_rank(class_ref, kind, rank, heads):
    found = jnp.int32(0)
    seen = jnp.int32(0)
    for head in range(heads):
        is_kind = class_ref[head] == kind
        found = jnp.where(is_kind & (seen == rank), head, found)
        seen = seen + is_kind.astype(jnp.int32)
    return found


def columns(index, width):
    return pl.ds(pl.multiple_of(index * width, width), width)


def head_copies(heads, width, kind, class_ref, sources, place, sems):
    copies = []
    for rank in range(heads // 2):
        head = head_of_rank(class_ref, kind, rank, heads)
        for index, source in enumerate(sources):
            copies.append(
                pltpu.make_async_copy(
                    source.at[:, columns(head, width)],
                    place(index, rank),
                    sems.at[index, rank],
                )
            )
    for copy in copies:
        copy.start()
    return copies


def pack_kernel(heads, width, class_ref, q_ref, k_ref, v_ref, packed_ref, sems):
    def place(index, rank):
        at = (index * (heads // 2) + rank) * width
        return packed_ref.at[:, at : at + width]

    for copy in head_copies(heads, width, 1, class_ref, (q_ref, k_ref, v_ref), place, sems):
        copy.wait()


def attend(queries, keys, values, listed, blocks):
    rows = queries.shape[0] // blocks
    scores = lax.dot_general(
        queries, keys, (((1,), (1,)), ((), ())), preferred_element_type=jnp.float32
    ) * (queries.shape[1] ** -0.5)
    key_block = lax.broadcasted_iota(jnp.int32, (rows, keys.shape[0]), 1) // rows
    masked = []
    for block in range(blocks):
        first, second = listed[block]
        allowed = (key_block == first) | (key_block == second)
        masked.append(
            jnp.where(allowed, scores[block * rows : (block + 1) * rows], -jnp.inf)
        )
    scores = jnp.concatenate(masked, axis=0)
    weights = jnp.exp(scores - jnp.max(scores, axis=1, keepdims=True))
    denominator = jnp.sum(weights, axis=1, keepdims=True)
    total = jnp.dot(
        weights.astype(jnp.bfloat16), values, preferred_element_type=jnp.float32
    )
    return (total / denominator).astype(jnp.bfloat16)


def lists_kernel(heads, blocks, lists_ref, counts_ref, out_ref):
    for head in range(heads):
        for block in range(blocks):
            first = lists_ref[head, 2 * block]
            second = jnp.where(counts_ref[head, block] > 1, lists_ref[head, 2 * block + 1], first)
            out_ref[head * blocks + block] = first * 256 + second


def listed_blocks(lists_ref, head, blocks):
    listed = []
    for block in range(blocks):
        both = lists_ref[head * blocks + block]
        listed.append((both >> 8, both & 255))
    return listed


def spatial_kernel(
    heads, width, blocks, class_ref, lists_ref, q_ref, k_ref, v_ref, out_ref, held_ref, sems
):
    copies = head_copies(
        heads,
        width,
        0,
        class_ref,
        (q_ref, k_ref, v_ref),
        lambda index, rank: held_ref.at[index, rank],
        sems,
    )
    for rank in range(heads // 2):
        head = head_of_rank(class_ref, 0, rank, heads)
        for copy in copies[3 * rank : 3 * rank + 3]:
            copy.wait()
        out_ref[:, rank * width : (rank + 1) * width] = attend(
            held_ref[0, rank],
            held_ref[1, rank],
            held_ref[2, rank],
            listed_blocks(lists_ref, head, blocks),
            blocks,
        )


def temporal_kernel(
    heads, width, blocks, class_ref, lists_ref, packed_ref, out_ref
):
    half = heads // 2
    for rank in range(half):
        head = head_of_rank(class_ref, 1, rank, heads)
        q, k, v = (
            packed_ref[:, (place * half + rank) * width : (place * half + rank + 1) * width]
            for place in range(3)
        )
        out_ref[:, rank * width : (rank + 1) * width] = attend(
            q, k, v, listed_blocks(lists_ref, head, blocks), blocks
        )


def place_heads(heads, width, class_ref, spatial_ref, temporal_ref, att_ref):
    rows = att_ref.shape[0] // 2
    side = lax.axis_index("head")
    for kind, ref in ((0, spatial_ref), (1, temporal_ref)):
        for rank in range(heads // 2):
            head = head_of_rank(class_ref, kind, rank, heads)
            for place, part in ((0, 1 - side), (1, side)):
                take = pl.ds(pl.multiple_of(part * rows, rows), rows)
                att_ref[place * rows : (place + 1) * rows, columns(head, width)] = ref[
                    take, rank * width : (rank + 1) * width
                ]


def project_pieces_kernel(heads, width, count, class_ref, spatial_ref, temporal_ref, *refs):
    pieces, (peer_ref, mine_ref, att_ref) = refs[: 2 * count], refs[2 * count :]
    place_heads(heads, width, class_ref, spatial_ref, temporal_ref, att_ref)
    depth, cols = pieces[0].shape
    rows = peer_ref.shape[0]
    half = lax.axis_index("groups")
    attended = jnp.concatenate(
        [att_ref[:, columns(half, depth)], att_ref[:, columns(1 - half, depth)]], axis=1
    )
    for index in range(0, count, 2):
        shards = range(index, min(index + 2, count))
        weight = jnp.concatenate(
            [
                jnp.concatenate([pieces[2 * at][...], pieces[2 * at + 1][...]], axis=0)
                for at in shards
            ],
            axis=1,
        )
        total = jnp.dot(attended, weight, preferred_element_type=jnp.float32)
        total = total.astype(peer_ref.dtype)
        take = slice(index * cols, (index + len(shards)) * cols)
        peer_ref[:, take] = total[:rows]
        mine_ref[:, take] = total[rows:]


def project_whole_kernel(
    heads, width, class_ref, spatial_ref, temporal_ref, weight_ref, peer_ref, mine_ref, att_ref
):
    place_heads(heads, width, class_ref, spatial_ref, temporal_ref, att_ref)
    rows = peer_ref.shape[0]
    for place, out_ref in enumerate((peer_ref, mine_ref)):
        out_ref[...] = jnp.dot(
            att_ref[place * rows : (place + 1) * rows, :],
            weight_ref[...],
            preferred_element_type=jnp.float32,
        ).astype(out_ref.dtype)


def join_kernel(shards, *refs):
    parts, out_ref = refs[:-1], refs[-1]
    index = lax.axis_index("frame")
    line, pair = index // 2, index % 2
    cols = out_ref.shape[1] // 8
    order = iter(shards)
    for mine_ref, received_ref in zip(parts[0::2], parts[1::2]):
        for at in range(mine_ref.shape[1] // cols):
            step, crossed = next(order)
            source = lax.rem(line - step + 4, 4) * 2 + (1 - pair if crossed else pair)
            take = slice(at * cols, (at + 1) * cols)
            total = mine_ref[:, take].astype(jnp.float32) + received_ref[:, take].astype(
                jnp.float32
            )
            out_ref[:, columns(source, cols)] = total.astype(out_ref.dtype)


def swap_pair(piece):
    return lax.ppermute(piece, "frame", [(i, i ^ 1) for i in range(8)])


def swap_group(piece):
    return lax.ppermute(piece, "groups", [(0, 1), (1, 0)])


def next_line(piece):
    return lax.ppermute(piece, "frame", [(i, (i + 2) % 8) for i in range(8)])


def swap_side(portion):
    return lax.ppermute(portion, "head", [(0, 1), (1, 0)])


def tied(*values):
    return lax.optimization_barrier(values)


def on_device(
    head_queries, head_keys, head_values, out_weight, head_class, block_lists, block_counts
):
    pixels = head_queries.shape[0]
    heads = head_class.shape[0]
    half = heads // 2
    width = head_queries.shape[1] // heads
    blocks = block_counts.shape[2]
    frames = lax.axis_size("frame")
    groups = lax.axis_size("groups")
    model = out_weight.shape[1] * frames
    bf16 = functools.partial(jax.ShapeDtypeStruct, dtype=jnp.bfloat16)
    def call(kernel, ins, outs, *operands, scratch=(), out_spec=VMEM):
        return pl.pallas_call(
            kernel,
            out_shape=outs,
            in_specs=ins,
            out_specs=jax.tree.map(lambda _: out_spec, outs),
            scratch_shapes=scratch,
            compiler_params=PARAMS,
            cost_estimate=pl.CostEstimate(flops=next(v for k, v in COSTS.items() if k in str(kernel)) * 10**6, bytes_accessed=1000, transcendentals=0),
        )(*operands)

    def exchange(rows):
        split = rows.reshape(frames, pixels // frames, rows.shape[1])
        return lax.all_to_all(
            split, "frame", split_axis=0, concat_axis=0, tiled=True
        ).reshape(rows.shape)

    lists = call(
        functools.partial(lists_kernel, heads, blocks),
        [SMEM, SMEM],
        jax.ShapeDtypeStruct((heads * blocks,), jnp.int32),
        block_lists.reshape(heads, -1),
        block_counts.reshape(heads, -1),
        out_spec=SMEM,
    )
    packed = call(
        functools.partial(pack_kernel, heads, width),
        [SMEM, ANY, ANY, ANY],
        bf16((pixels, 3 * half * width)),
        head_class,
        head_queries,
        head_keys,
        head_values,
        scratch=[pltpu.SemaphoreType.DMA((3, half))],
    )

    def spatial_heads():
        return call(
            functools.partial(spatial_kernel, heads, width, blocks),
            [SMEM, SMEM, ANY, ANY, ANY],
            bf16((pixels, half * width)),
            head_class,
            lists,
            head_queries,
            head_keys,
            head_values,
            scratch=[
                pltpu.VMEM((3, half, pixels, width), jnp.bfloat16),
                pltpu.SemaphoreType.DMA((3, half)),
            ],
        )

    def temporal_heads(arrived):
        return call(
            functools.partial(temporal_kernel, heads, width, blocks),
            [SMEM, SMEM, VMEM],
            bf16((pixels, half * width)),
            head_class,
            lists,
            arrived,
        )

    att_scratch = [pltpu.VMEM((pixels, heads * width), jnp.bfloat16)]
    if frames != 8 or groups != 2:
        spatial = spatial_heads()
        returned = exchange(temporal_heads(exchange(packed)))
        weight = lax.all_gather(out_weight, "frame", axis=1, tiled=True)
        peer, mine = call(
            functools.partial(project_whole_kernel, heads, width),
            [SMEM, VMEM, VMEM, VMEM],
            [bf16((pixels // 2, model))] * 2,
            head_class,
            spatial,
            returned,
            weight,
            scratch=att_scratch,
        )
        received = swap_side(peer)
        return (mine.astype(jnp.float32) + received.astype(jnp.float32)).astype(jnp.bfloat16)

    depth, cols = out_weight.shape[0] // 2, out_weight.shape[1]
    group = lax.axis_index("groups")
    own = lax.dynamic_slice_in_dim(out_weight, group * depth, depth, 0)
    rest = lax.dynamic_slice_in_dim(out_weight, (1 - group) * depth, depth, 0)

    def project(pieces):
        count = len(pieces) // 2
        return call(
            functools.partial(project_pieces_kernel, heads, width, count),
            [SMEM] + [VMEM] * (2 + len(pieces)),
            [bf16((pixels // 2, count * cols))] * 2,
            head_class,
            spatial,
            returned,
            *pieces,
            scratch=att_scratch,
        )

    arrived = exchange(packed)
    held_1, pair_0, lists = tied(next_line(own), swap_pair(own), lists)
    pair_1, rest_1, pair_rest_0, spatial = tied(
        swap_pair(held_1), swap_group(held_1), swap_group(pair_0), spatial_heads()
    )
    pair_rest_1 = swap_group(pair_1)
    held_2, arrived = tied(next_line(held_1), arrived)
    returned = exchange(temporal_heads(arrived))
    held_3, pair_2, rest_2, pair_rest_1 = tied(
        next_line(held_2), swap_pair(held_2), swap_group(held_2), pair_rest_1
    )
    pair_3, rest_3, returned, pair_2 = tied(
        swap_pair(held_3), swap_group(held_3), returned, pair_2
    )
    pair_rest_2, pair_rest_3 = swap_group(pair_2), swap_pair(rest_3)
    peer, mine = project(
        [own, rest, pair_0, pair_rest_0, held_1, rest_1, pair_1, pair_rest_1, held_2, rest_2]
        + [held_3, rest_3]
    )
    received = swap_side(peer)
    last_peer, last_mine = project([pair_2, pair_rest_2, pair_3, pair_rest_3])
    last_received = swap_side(last_peer)
    order = ((0, 0), (0, 1), (1, 0), (1, 1), (2, 0), (3, 0), (2, 1), (3, 1))
    return call(
        functools.partial(join_kernel, order),
        [VMEM] * 4,
        bf16((pixels // 2, model)),
        mine,
        received,
        last_mine,
        last_received,
    )


def solution(mesh):
    placed = (
        P(("groups", "frame"), "head"),
        P(("groups", "frame"), "head"),
        P(("groups", "frame"), "head"),
        P("head", "frame"),
        P("head"),
        P("head", ("groups", "frame"), None, None),
        P("head", ("groups", "frame"), None),
    )
    return jax.shard_map(
        on_device,
        mesh=mesh,
        in_specs=placed,
        out_specs=P(("groups", "frame", "head"), None),
        check_vma=False,
    )
```

```python
import functools

import jax
import jax.numpy as jnp
from jax import lax
from jax.experimental import pallas as pl
from jax.experimental.pallas import tpu as pltpu
from jax.sharding import PartitionSpec as P

VMEM = pl.BlockSpec(memory_space=pltpu.VMEM)
SMEM = pl.BlockSpec(memory_space=pltpu.SMEM)
ANY = pl.BlockSpec(memory_space=pl.ANY)
HBM = pl.BlockSpec(memory_space=pltpu.HBM)
COSTS = {"pack": 5000, "spatial": 10000, "temporal": 5000, "join_first": 1, "join_last": 1, "project_first": 3000, "project_last": 5000, "project_whole": 20000}
PARAMS = pltpu.CompilerParams(vmem_limit_bytes=16 * 1024 * 1024)


def head_of_rank(class_ref, kind, rank, heads):
    found = jnp.int32(0)
    seen = jnp.int32(0)
    for head in range(heads):
        is_kind = class_ref[head] == kind
        found = jnp.where(is_kind & (seen == rank), head, found)
        seen = seen + is_kind.astype(jnp.int32)
    return found


def columns(index, width):
    return pl.ds(pl.multiple_of(index * width, width), width)


def head_copies(heads, width, kind, class_ref, sources, place, sems):
    copies = []
    for rank in range(heads // 2):
        head = head_of_rank(class_ref, kind, rank, heads)
        for index, source in enumerate(sources):
            copies.append(
                pltpu.make_async_copy(
                    source.at[:, columns(head, width)],
                    place(index, rank),
                    sems.at[index, rank],
                )
            )
    for copy in copies:
        copy.start()
    return copies


def pack_kernel(heads, width, class_ref, q_ref, k_ref, v_ref, packed_ref, sems):
    def place(index, rank):
        at = (index * (heads // 2) + rank) * width
        return packed_ref.at[:, at : at + width]

    for copy in head_copies(heads, width, 1, class_ref, (q_ref, k_ref, v_ref), place, sems):
        copy.wait()


def attend(load, head, lists_ref, counts_ref, blocks):
    queries, keys, values = (load(place) for place in range(3))
    rows = queries.shape[0] // blocks
    scores = lax.dot_general(
        queries, keys, (((1,), (1,)), ((), ())), preferred_element_type=jnp.float32
    ) * (queries.shape[1] ** -0.5)
    key_block = lax.broadcasted_iota(jnp.int32, (rows, keys.shape[0]), 1) // rows
    masked = []
    for block in range(blocks):
        first = lists_ref[head, 2 * block]
        second = lists_ref[head, 2 * block + 1]
        second = jnp.where(counts_ref[head, block] > 1, second, first)
        allowed = (key_block == first) | (key_block == second)
        masked.append(
            jnp.where(allowed, scores[block * rows : (block + 1) * rows], -jnp.inf)
        )
    scores = jnp.concatenate(masked, axis=0)
    weights = jnp.exp(scores - jnp.max(scores, axis=1, keepdims=True))
    denominator = jnp.sum(weights, axis=1, keepdims=True)
    total = jnp.dot(
        weights.astype(jnp.bfloat16), values, preferred_element_type=jnp.float32
    )
    return (total / denominator).astype(jnp.bfloat16)


def spatial_kernel(
    heads,
    width,
    blocks,
    class_ref,
    lists_ref,
    counts_ref,
    q_ref,
    k_ref,
    v_ref,
    out_ref,
    held_ref,
    sems,
):
    copies = head_copies(
        heads,
        width,
        0,
        class_ref,
        (q_ref, k_ref, v_ref),
        lambda index, rank: held_ref.at[index, rank],
        sems,
    )
    for rank in range(heads // 2):
        head = head_of_rank(class_ref, 0, rank, heads)
        for copy in copies[3 * rank : 3 * rank + 3]:
            copy.wait()
        out_ref[:, rank * width : (rank + 1) * width] = attend(
            lambda place: held_ref[place, rank],
            head,
            lists_ref,
            counts_ref,
            blocks,
        )


def temporal_kernel(
    heads, width, blocks, class_ref, lists_ref, counts_ref, packed_ref, out_ref
):
    half = heads // 2
    for rank in range(half):
        head = head_of_rank(class_ref, 1, rank, heads)

        def load(place):
            at = (place * half + rank) * width
            return packed_ref[:, at : at + width]

        out_ref[:, rank * width : (rank + 1) * width] = attend(
            load, head, lists_ref, counts_ref, blocks
        )


def place_heads(heads, width, class_ref, spatial_ref, temporal_ref, att_ref):
    rows = att_ref.shape[0] // 2
    side = lax.axis_index("head")
    for kind, ref in ((0, spatial_ref), (1, temporal_ref)):
        for rank in range(heads // 2):
            head = head_of_rank(class_ref, kind, rank, heads)
            for place, part in ((0, 1 - side), (1, side)):
                take = pl.ds(pl.multiple_of(part * rows, rows), rows)
                att_ref[place * rows : (place + 1) * rows, columns(head, width)] = ref[
                    take, rank * width : (rank + 1) * width
                ]


def project_pieces(attended, pieces, peer_ref, mine_ref):
    rows, cols = peer_ref.shape[0], pieces[0].shape[1]
    for index in range(0, len(pieces), 4):
        weight = jnp.concatenate(
            [
                jnp.concatenate([piece[...] for piece in pieces[at : at + 2]], axis=0)
                for at in range(index, index + 4, 2)
            ],
            axis=1,
        )
        total = jnp.dot(attended, weight, preferred_element_type=jnp.float32)
        total = total.astype(peer_ref.dtype)
        take = slice(index // 2 * cols, (index // 2 + 2) * cols)
        peer_ref[:, take] = total[:rows]
        mine_ref[:, take] = total[rows:]


def project_first_kernel(heads, width, class_ref, spatial_ref, temporal_ref, *refs):
    pieces, (peer_ref, mine_ref, attended_ref, att_ref) = refs[:-4], refs[-4:]
    place_heads(heads, width, class_ref, spatial_ref, temporal_ref, att_ref)
    depth = pieces[0].shape[0]
    half = lax.axis_index("groups")
    halves = (columns(half, depth), columns(1 - half, depth))
    for at, side in enumerate(halves):
        attended_ref[:, at * depth : (at + 1) * depth] = att_ref[:, side]
    project_pieces(attended_ref[...], pieces, peer_ref, mine_ref)


def project_last_kernel(attended_ref, *refs):
    pieces, (peer_ref, mine_ref) = refs[:-2], refs[-2:]
    project_pieces(attended_ref[...], pieces, peer_ref, mine_ref)


def project_whole_kernel(
    heads, width, class_ref, spatial_ref, temporal_ref, weight_ref, peer_ref, mine_ref, att_ref
):
    place_heads(heads, width, class_ref, spatial_ref, temporal_ref, att_ref)
    rows = peer_ref.shape[0]
    for place, out_ref in enumerate((peer_ref, mine_ref)):
        out_ref[...] = jnp.dot(
            att_ref[place * rows : (place + 1) * rows, :],
            weight_ref[...],
            preferred_element_type=jnp.float32,
        ).astype(out_ref.dtype)


def join_shards(shards, mine_ref, received_ref, out_ref, held_ref, sems):
    index = lax.axis_index("frame")
    line, pair = index // 2, lax.rem(index, 2)
    cols = mine_ref.shape[1] // len(shards)
    copies = []
    for at, (step, crossed) in enumerate(shards):
        source = lax.rem(line - step + 4, 4) * 2 + (1 - pair if crossed else pair)
        take = slice(at * cols, (at + 1) * cols)
        held_ref[:, take] = (
            mine_ref[:, take].astype(jnp.float32) + received_ref[:, take].astype(jnp.float32)
        ).astype(out_ref.dtype)
        copies.append(
            pltpu.make_async_copy(
                held_ref.at[:, take], out_ref.at[:, columns(source, cols)], sems.at[at]
            )
        )
        copies[-1].start()
    for copy in copies:
        copy.wait()


def join_first_kernel(shards, *refs):
    join_shards(shards, *refs)


def join_last_kernel(shards, mine_ref, received_ref, joined_ref, *refs):
    join_shards(shards, mine_ref, received_ref, *refs)


def swap_pair(piece):
    return lax.ppermute(piece, "frame", [(i, i ^ 1) for i in range(8)])


def swap_group(piece):
    return lax.ppermute(piece, "groups", [(0, 1), (1, 0)])


def next_line(piece):
    return lax.ppermute(piece, "frame", [(i, (i + 2) % 8) for i in range(8)])


def swap_side(portion):
    return lax.ppermute(portion, "head", [(0, 1), (1, 0)])


def tied(*values):
    return lax.optimization_barrier(values)


def on_device(
    head_queries, head_keys, head_values, out_weight, head_class, block_lists, block_counts
):
    pixels = head_queries.shape[0]
    heads = head_class.shape[0]
    half = heads // 2
    width = head_queries.shape[1] // heads
    blocks = block_counts.shape[2]
    frames = lax.axis_size("frame")
    groups = lax.axis_size("groups")
    model = out_weight.shape[1] * frames
    bf16 = functools.partial(jax.ShapeDtypeStruct, dtype=jnp.bfloat16)
    def call(kernel, ins, outs, *operands, scratch=(), out_spec=VMEM, aliases={}):
        return pl.pallas_call(
            kernel,
            out_shape=outs,
            in_specs=ins,
            out_specs=jax.tree.map(lambda _: out_spec, outs),
            input_output_aliases=aliases,
            scratch_shapes=scratch,
            compiler_params=PARAMS,
            cost_estimate=pl.CostEstimate(flops=next(v for k, v in COSTS.items() if k in str(kernel)) * 10**6, bytes_accessed=1000, transcendentals=0),
        )(*operands)

    def exchange(rows):
        split = rows.reshape(frames, pixels // frames, rows.shape[1])
        return lax.all_to_all(
            split, "frame", split_axis=0, concat_axis=0, tiled=True
        ).reshape(rows.shape)

    lists = (block_lists.reshape(heads, -1), block_counts.reshape(heads, -1))
    packed = call(
        functools.partial(pack_kernel, heads, width),
        [SMEM, ANY, ANY, ANY],
        bf16((pixels, 3 * half * width)),
        head_class,
        head_queries,
        head_keys,
        head_values,
        scratch=[pltpu.SemaphoreType.DMA((3, half))],
    )

    def spatial_heads():
        return call(
            functools.partial(spatial_kernel, heads, width, blocks),
            [SMEM, SMEM, SMEM, ANY, ANY, ANY],
            bf16((pixels, half * width)),
            head_class,
            *lists,
            head_queries,
            head_keys,
            head_values,
            scratch=[
                pltpu.VMEM((3, half, pixels, width), jnp.bfloat16),
                pltpu.SemaphoreType.DMA((3, half)),
            ],
        )

    def temporal_heads(arrived):
        return call(
            functools.partial(temporal_kernel, heads, width, blocks),
            [SMEM, SMEM, SMEM, VMEM],
            bf16((pixels, half * width)),
            head_class,
            *lists,
            arrived,
        )

    att_scratch = [pltpu.VMEM((pixels, heads * width), jnp.bfloat16)]
    if frames != 8 or groups != 2:
        spatial = spatial_heads()
        returned = exchange(temporal_heads(exchange(packed)))
        weight = lax.all_gather(out_weight, "frame", axis=1, tiled=True)
        peer, mine = call(
            functools.partial(project_whole_kernel, heads, width),
            [SMEM, VMEM, VMEM, VMEM],
            [bf16((pixels // 2, model))] * 2,
            head_class,
            spatial,
            returned,
            weight,
            scratch=att_scratch,
        )
        received = swap_side(peer)
        return (mine.astype(jnp.float32) + received.astype(jnp.float32)).astype(jnp.bfloat16)

    depth, cols = out_weight.shape[0] // 2, out_weight.shape[1]
    group = lax.axis_index("groups")
    own = lax.dynamic_slice_in_dim(out_weight, group * depth, depth, 0)
    rest = lax.dynamic_slice_in_dim(out_weight, (1 - group) * depth, depth, 0)

    def join(kernel, shards, mine, received, joined=None):
        return call(
            functools.partial(kernel, shards),
            [VMEM, VMEM] + ([] if joined is None else [HBM]),
            bf16((pixels // 2, model)),
            mine,
            received,
            *([] if joined is None else [joined]),
            scratch=[
                pltpu.VMEM(mine.shape, jnp.bfloat16),
                pltpu.SemaphoreType.DMA((len(shards),)),
            ],
            out_spec=HBM,
            aliases={} if joined is None else {2: 0},
        )

    arrived = exchange(packed)
    held_1, pair_0 = tied(next_line(own), swap_pair(own))
    pair_1, rest_1, pair_rest_0, spatial = tied(
        swap_pair(held_1), swap_group(held_1), swap_group(pair_0), spatial_heads()
    )
    pair_rest_1 = swap_group(pair_1)
    held_2 = next_line(held_1)
    returned = exchange(temporal_heads(arrived))
    held_3, pair_2, rest_2, pair_rest_1 = tied(
        next_line(held_2), swap_pair(held_2), swap_group(held_2), pair_rest_1
    )
    pair_3, rest_3, returned, pair_2 = tied(
        swap_pair(held_3), swap_group(held_3), returned, pair_2
    )
    pair_rest_2, pair_rest_3 = swap_group(pair_2), swap_pair(rest_3)
    pieces = [own, rest, pair_0, pair_rest_0, held_1, rest_1, pair_1, pair_rest_1]
    pieces += [held_2, rest_2, held_3, rest_3]
    peer, mine, attended = call(
        functools.partial(project_first_kernel, heads, width),
        [SMEM] + [VMEM] * (2 + len(pieces)),
        [bf16((pixels // 2, 6 * cols))] * 2 + [bf16((pixels, heads * width))],
        head_class,
        spatial,
        returned,
        *pieces,
        scratch=att_scratch,
    )
    received = swap_side(peer)
    last_peer, last_mine = call(
        project_last_kernel,
        [VMEM] * 5,
        [bf16((pixels // 2, 2 * cols))] * 2,
        attended,
        pair_2,
        pair_rest_2,
        pair_3,
        pair_rest_3,
    )
    last_received = swap_side(last_peer)
    joined = join(
        join_first_kernel, ((0, 0), (0, 1), (1, 0), (1, 1), (2, 0), (3, 0)), mine, received
    )
    return join(join_last_kernel, ((2, 1), (3, 1)), last_mine, last_received, joined)


def solution(mesh):
    placed = (
        P(("groups", "frame"), "head"),
        P(("groups", "frame"), "head"),
        P(("groups", "frame"), "head"),
        P("head", "frame"),
        P("head"),
        P("head", ("groups", "frame"), None, None),
        P("head", ("groups", "frame"), None),
    )
    return jax.shard_map(
        on_device,
        mesh=mesh,
        in_specs=placed,
        out_specs=P(("groups", "frame", "head"), None),
        check_vma=False,
    )
```

```python
import functools

import jax
import jax.numpy as jnp
from jax import lax
from jax.experimental import pallas as pl
from jax.experimental.pallas import tpu as pltpu
from jax.sharding import PartitionSpec as P

VMEM = pl.BlockSpec(memory_space=pltpu.VMEM)
SMEM = pl.BlockSpec(memory_space=pltpu.SMEM)
ANY = pl.BlockSpec(memory_space=pl.ANY)
HBM = pl.BlockSpec(memory_space=pltpu.HBM)
PARAMS = pltpu.CompilerParams(vmem_limit_bytes=16 * 1024 * 1024)


def head_of_rank(class_ref, kind, rank, heads):
    found = jnp.int32(0)
    seen = jnp.int32(0)
    for head in range(heads):
        is_kind = class_ref[head] == kind
        found = jnp.where(is_kind & (seen == rank), head, found)
        seen = seen + is_kind.astype(jnp.int32)
    return found


def columns(index, width):
    return pl.ds(pl.multiple_of(index * width, width), width)


def head_copies(heads, width, kind, class_ref, sources, place, sems):
    copies = []
    for rank in range(heads // 2):
        head = head_of_rank(class_ref, kind, rank, heads)
        for index, source in enumerate(sources):
            copies.append(
                pltpu.make_async_copy(
                    source.at[:, columns(head, width)],
                    place(index, rank),
                    sems.at[index, rank],
                )
            )
    for copy in copies:
        copy.start()
    return copies


def pack_kernel(heads, width, class_ref, q_ref, k_ref, v_ref, packed_ref, sems):
    def place(index, rank):
        at = (index * (heads // 2) + rank) * width
        return packed_ref.at[:, at : at + width]

    for copy in head_copies(heads, width, 1, class_ref, (q_ref, k_ref, v_ref), place, sems):
        copy.wait()


def attend(load, head, lists_ref, counts_ref, blocks):
    queries, keys, values = (load(place) for place in range(3))
    rows = queries.shape[0] // blocks
    scores = lax.dot_general(
        queries, keys, (((1,), (1,)), ((), ())), preferred_element_type=jnp.float32
    ) * (queries.shape[1] ** -0.5)
    key_block = lax.broadcasted_iota(jnp.int32, (rows, keys.shape[0]), 1) // rows
    masked = []
    for block in range(blocks):
        first = lists_ref[head, 2 * block]
        second = lists_ref[head, 2 * block + 1]
        second = jnp.where(counts_ref[head, block] > 1, second, first)
        allowed = (key_block == first) | (key_block == second)
        masked.append(
            jnp.where(allowed, scores[block * rows : (block + 1) * rows], -jnp.inf)
        )
    scores = jnp.concatenate(masked, axis=0)
    weights = jnp.exp(scores - jnp.max(scores, axis=1, keepdims=True))
    denominator = jnp.sum(weights, axis=1, keepdims=True)
    total = jnp.dot(
        weights.astype(jnp.bfloat16), values, preferred_element_type=jnp.float32
    )
    return (total / denominator).astype(jnp.bfloat16)


def spatial_kernel(
    heads,
    width,
    blocks,
    class_ref,
    lists_ref,
    counts_ref,
    q_ref,
    k_ref,
    v_ref,
    out_ref,
    held_ref,
    sems,
):
    copies = head_copies(
        heads,
        width,
        0,
        class_ref,
        (q_ref, k_ref, v_ref),
        lambda index, rank: held_ref.at[index, rank],
        sems,
    )
    for rank in range(heads // 2):
        head = head_of_rank(class_ref, 0, rank, heads)
        for copy in copies[3 * rank : 3 * rank + 3]:
            copy.wait()
        out_ref[:, rank * width : (rank + 1) * width] = attend(
            lambda place: held_ref[place, rank],
            head,
            lists_ref,
            counts_ref,
            blocks,
        )


def temporal_kernel(
    heads, width, blocks, class_ref, lists_ref, counts_ref, packed_ref, out_ref
):
    half = heads // 2
    for rank in range(half):
        head = head_of_rank(class_ref, 1, rank, heads)

        def load(place):
            at = (place * half + rank) * width
            return packed_ref[:, at : at + width]

        out_ref[:, rank * width : (rank + 1) * width] = attend(
            load, head, lists_ref, counts_ref, blocks
        )


def place_heads(heads, width, class_ref, spatial_ref, temporal_ref, att_ref):
    rows = att_ref.shape[0] // 2
    side = lax.axis_index("head")
    for kind, ref in ((0, spatial_ref), (1, temporal_ref)):
        for rank in range(heads // 2):
            head = head_of_rank(class_ref, kind, rank, heads)
            for place, part in ((0, 1 - side), (1, side)):
                take = pl.ds(pl.multiple_of(part * rows, rows), rows)
                att_ref[place * rows : (place + 1) * rows, columns(head, width)] = ref[
                    take, rank * width : (rank + 1) * width
                ]


def project_pieces(attended, pieces, peer_ref, mine_ref):
    rows, cols = peer_ref.shape[0], pieces[0].shape[1]
    for index in range(0, len(pieces), 4):
        weight = jnp.concatenate(
            [
                jnp.concatenate([piece[...] for piece in pieces[at : at + 2]], axis=0)
                for at in range(index, index + 4, 2)
            ],
            axis=1,
        )
        total = jnp.dot(attended, weight, preferred_element_type=jnp.float32)
        total = total.astype(peer_ref.dtype)
        take = slice(index // 2 * cols, (index // 2 + 2) * cols)
        peer_ref[:, take] = total[:rows]
        mine_ref[:, take] = total[rows:]


def project_first_kernel(heads, width, class_ref, spatial_ref, temporal_ref, *refs):
    pieces, (peer_ref, mine_ref, attended_ref, att_ref) = refs[:-4], refs[-4:]
    place_heads(heads, width, class_ref, spatial_ref, temporal_ref, att_ref)
    depth = pieces[0].shape[0]
    half = lax.axis_index("groups")
    halves = (columns(half, depth), columns(1 - half, depth))
    for at, side in enumerate(halves):
        attended_ref[:, at * depth : (at + 1) * depth] = att_ref[:, side]
    project_pieces(attended_ref[...], pieces, peer_ref, mine_ref)


def project_last_kernel(attended_ref, *refs):
    pieces, (peer_ref, mine_ref) = refs[:-2], refs[-2:]
    project_pieces(attended_ref[...], pieces, peer_ref, mine_ref)


def project_whole_kernel(
    heads, width, class_ref, spatial_ref, temporal_ref, weight_ref, peer_ref, mine_ref, att_ref
):
    place_heads(heads, width, class_ref, spatial_ref, temporal_ref, att_ref)
    rows = peer_ref.shape[0]
    for place, out_ref in enumerate((peer_ref, mine_ref)):
        out_ref[...] = jnp.dot(
            att_ref[place * rows : (place + 1) * rows, :],
            weight_ref[...],
            preferred_element_type=jnp.float32,
        ).astype(out_ref.dtype)


def join_shards(shards, mine_ref, received_ref, out_ref, held_ref, sems):
    index = lax.axis_index("frame")
    line, pair = index // 2, lax.rem(index, 2)
    cols = mine_ref.shape[1] // len(shards)
    copies = []
    for at, (step, crossed) in enumerate(shards):
        source = lax.rem(line - step + 4, 4) * 2 + (1 - pair if crossed else pair)
        take = slice(at * cols, (at + 1) * cols)
        held_ref[:, take] = (
            mine_ref[:, take].astype(jnp.float32) + received_ref[:, take].astype(jnp.float32)
        ).astype(out_ref.dtype)
        copies.append(
            pltpu.make_async_copy(
                held_ref.at[:, take], out_ref.at[:, columns(source, cols)], sems.at[at]
            )
        )
        copies[-1].start()
    for copy in copies:
        copy.wait()


def join_first_kernel(shards, *refs):
    join_shards(shards, *refs)


def join_last_kernel(shards, mine_ref, received_ref, joined_ref, *refs):
    join_shards(shards, mine_ref, received_ref, *refs)


def swap_pair(piece):
    return lax.ppermute(piece, "frame", [(i, i ^ 1) for i in range(8)])


def swap_group(piece):
    return lax.ppermute(piece, "groups", [(0, 1), (1, 0)])


def next_line(piece):
    return lax.ppermute(piece, "frame", [(i, (i + 2) % 8) for i in range(8)])


def swap_side(portion):
    return lax.ppermute(portion, "head", [(0, 1), (1, 0)])


def tied(*values):
    return lax.optimization_barrier(values)


def on_device(
    head_queries, head_keys, head_values, out_weight, head_class, block_lists, block_counts
):
    pixels = head_queries.shape[0]
    heads = head_class.shape[0]
    half = heads // 2
    width = head_queries.shape[1] // heads
    blocks = block_counts.shape[2]
    frames = lax.axis_size("frame")
    groups = lax.axis_size("groups")
    model = out_weight.shape[1] * frames
    bf16 = functools.partial(jax.ShapeDtypeStruct, dtype=jnp.bfloat16)
    def call(work, kernel, ins, outs, *operands, scratch=(), out_spec=VMEM, aliases={}):
        return pl.pallas_call(
            kernel,
            out_shape=outs,
            in_specs=ins,
            out_specs=jax.tree.map(lambda _: out_spec, outs),
            input_output_aliases=aliases,
            scratch_shapes=scratch,
            compiler_params=PARAMS,
            cost_estimate=pl.CostEstimate(flops=work * 10**6, bytes_accessed=1000, transcendentals=0),
        )(*operands)

    def exchange(rows):
        split = rows.reshape(frames, pixels // frames, rows.shape[1])
        return lax.all_to_all(
            split, "frame", split_axis=0, concat_axis=0, tiled=True
        ).reshape(rows.shape)

    lists = (block_lists.reshape(heads, -1), block_counts.reshape(heads, -1))
    packed = call(
        5000,
        functools.partial(pack_kernel, heads, width),
        [SMEM, ANY, ANY, ANY],
        bf16((pixels, 3 * half * width)),
        head_class,
        head_queries,
        head_keys,
        head_values,
        scratch=[pltpu.SemaphoreType.DMA((3, half))],
    )

    def spatial_heads():
        return call(
            10000,
            functools.partial(spatial_kernel, heads, width, blocks),
            [SMEM, SMEM, SMEM, ANY, ANY, ANY],
            bf16((pixels, half * width)),
            head_class,
            *lists,
            head_queries,
            head_keys,
            head_values,
            scratch=[
                pltpu.VMEM((3, half, pixels, width), jnp.bfloat16),
                pltpu.SemaphoreType.DMA((3, half)),
            ],
        )

    def temporal_heads(arrived):
        return call(
            5000,
            functools.partial(temporal_kernel, heads, width, blocks),
            [SMEM, SMEM, SMEM, VMEM],
            bf16((pixels, half * width)),
            head_class,
            *lists,
            arrived,
        )

    att_scratch = [pltpu.VMEM((pixels, heads * width), jnp.bfloat16)]
    if frames != 8 or groups != 2:
        spatial = spatial_heads()
        returned = exchange(temporal_heads(exchange(packed)))
        weight = lax.all_gather(out_weight, "frame", axis=1, tiled=True)
        peer, mine = call(
            20000,
            functools.partial(project_whole_kernel, heads, width),
            [SMEM, VMEM, VMEM, VMEM],
            [bf16((pixels // 2, model))] * 2,
            head_class,
            spatial,
            returned,
            weight,
            scratch=att_scratch,
        )
        received = swap_side(peer)
        return (mine.astype(jnp.float32) + received.astype(jnp.float32)).astype(jnp.bfloat16)

    depth, cols = out_weight.shape[0] // 2, out_weight.shape[1]
    group = lax.axis_index("groups")
    own = lax.dynamic_slice_in_dim(out_weight, group * depth, depth, 0)
    rest = lax.dynamic_slice_in_dim(out_weight, (1 - group) * depth, depth, 0)

    def join(kernel, shards, mine, received, joined=None):
        return call(
            1,
            functools.partial(kernel, shards),
            [VMEM, VMEM] + ([] if joined is None else [HBM]),
            bf16((pixels // 2, model)),
            mine,
            received,
            *([] if joined is None else [joined]),
            scratch=[
                pltpu.VMEM(mine.shape, jnp.bfloat16),
                pltpu.SemaphoreType.DMA((len(shards),)),
            ],
            out_spec=HBM,
            aliases={} if joined is None else {2: 0},
        )

    arrived = exchange(packed)
    pair_0, held_1 = tied(swap_pair(own), next_line(own))
    pair_1, rest_1, pair_rest_0, spatial = tied(
        swap_pair(held_1), swap_group(held_1), swap_group(pair_0), spatial_heads()
    )
    pair_rest_1 = swap_group(pair_1)
    held_2 = next_line(held_1)
    returned = exchange(temporal_heads(arrived))
    held_3, pair_2, rest_2, pair_rest_1 = tied(
        next_line(held_2), swap_pair(held_2), swap_group(held_2), pair_rest_1
    )
    pair_3, rest_3, returned, pair_2 = tied(
        swap_pair(held_3), swap_group(held_3), returned, pair_2
    )
    pair_rest_2, pair_rest_3 = swap_group(pair_2), swap_pair(rest_3)
    pieces = [own, rest, pair_0, pair_rest_0, held_1, rest_1, pair_1, pair_rest_1]
    pieces += [held_2, rest_2, held_3, rest_3]
    peer, mine, attended = call(
        3000,
        functools.partial(project_first_kernel, heads, width),
        [SMEM] + [VMEM] * (2 + len(pieces)),
        [bf16((pixels // 2, 6 * cols))] * 2 + [bf16((pixels, heads * width))],
        head_class,
        spatial,
        returned,
        *pieces,
        scratch=att_scratch,
    )
    received = swap_side(peer)
    last_peer, last_mine = call(
        5000,
        project_last_kernel,
        [VMEM] * 5,
        [bf16((pixels // 2, 2 * cols))] * 2,
        attended,
        pair_2,
        pair_rest_2,
        pair_3,
        pair_rest_3,
    )
    last_received = swap_side(last_peer)
    joined = join(
        join_first_kernel, ((0, 0), (0, 1), (1, 0), (1, 1), (2, 0), (3, 0)), mine, received
    )
    return join(join_last_kernel, ((2, 1), (3, 1)), last_mine, last_received, joined)


def solution(mesh):
    placed = (
        P(("groups", "frame"), "head"),
        P(("groups", "frame"), "head"),
        P(("groups", "frame"), "head"),
        P("head", "frame"),
        P("head"),
        P("head", ("groups", "frame"), None, None),
        P("head", ("groups", "frame"), None),
    )
    return jax.shard_map(
        on_device,
        mesh=mesh,
        in_specs=placed,
        out_specs=P(("groups", "frame", "head"), None),
        check_vma=False,
    )
```

```python
import functools

import jax
import jax.numpy as jnp
from jax import lax
from jax.experimental import pallas as pl
from jax.experimental.pallas import tpu as pltpu
from jax.sharding import PartitionSpec as P

VMEM = pl.BlockSpec(memory_space=pltpu.VMEM)
SMEM = pl.BlockSpec(memory_space=pltpu.SMEM)
ANY = pl.BlockSpec(memory_space=pl.ANY)
HBM = pl.BlockSpec(memory_space=pltpu.HBM)
COSTS = {"pack": 5000, "spatial": 10000, "temporal": 5000, "join_first": 1, "join_last": 1, "project_first": 3000, "project_last": 5000, "project_whole": 20000}
PARAMS = pltpu.CompilerParams(vmem_limit_bytes=10 * 1024 * 1024)


def head_of_rank(class_ref, kind, rank, heads):
    found = jnp.int32(0)
    seen = jnp.int32(0)
    for head in range(heads):
        is_kind = class_ref[head] == kind
        found = jnp.where(is_kind & (seen == rank), head, found)
        seen = seen + is_kind.astype(jnp.int32)
    return found


def columns(index, width):
    return pl.ds(pl.multiple_of(index * width, width), width)


def head_copies(heads, width, kind, class_ref, sources, place, sems):
    copies = []
    for rank in range(heads // 2):
        head = head_of_rank(class_ref, kind, rank, heads)
        for index, source in enumerate(sources):
            copies.append(
                pltpu.make_async_copy(
                    source.at[:, columns(head, width)],
                    place(index, rank),
                    sems.at[index, rank],
                )
            )
    for copy in copies:
        copy.start()
    return copies


def pack_kernel(heads, width, class_ref, q_ref, k_ref, v_ref, packed_ref, sems):
    def place(index, rank):
        at = (index * (heads // 2) + rank) * width
        return packed_ref.at[:, at : at + width]

    for copy in head_copies(heads, width, 1, class_ref, (q_ref, k_ref, v_ref), place, sems):
        copy.wait()


def attend(load, head, lists_ref, counts_ref, blocks):
    queries, keys, values = (load(place) for place in range(3))
    rows = queries.shape[0] // blocks
    scores = lax.dot_general(
        queries, keys, (((1,), (1,)), ((), ())), preferred_element_type=jnp.float32
    ) * (queries.shape[1] ** -0.5)
    key_block = lax.broadcasted_iota(jnp.int32, (rows, keys.shape[0]), 1) // rows
    masked = []
    for block in range(blocks):
        first = lists_ref[head, 2 * block]
        second = lists_ref[head, 2 * block + 1]
        second = jnp.where(counts_ref[head, block] > 1, second, first)
        allowed = (key_block == first) | (key_block == second)
        masked.append(
            jnp.where(allowed, scores[block * rows : (block + 1) * rows], -jnp.inf)
        )
    scores = jnp.concatenate(masked, axis=0)
    weights = jnp.exp(scores - jnp.max(scores, axis=1, keepdims=True))
    denominator = jnp.sum(weights, axis=1, keepdims=True)
    total = jnp.dot(
        weights.astype(jnp.bfloat16), values, preferred_element_type=jnp.float32
    )
    return (total * (1.0 / denominator)).astype(jnp.bfloat16)


def spatial_kernel(
    heads,
    width,
    blocks,
    class_ref,
    lists_ref,
    counts_ref,
    q_ref,
    k_ref,
    v_ref,
    out_ref,
    held_ref,
    sems,
):
    copies = head_copies(
        heads,
        width,
        0,
        class_ref,
        (q_ref, k_ref, v_ref),
        lambda index, rank: held_ref.at[index, rank],
        sems,
    )
    for rank in range(heads // 2):
        head = head_of_rank(class_ref, 0, rank, heads)
        for copy in copies[3 * rank : 3 * rank + 3]:
            copy.wait()
        out_ref[:, rank * width : (rank + 1) * width] = attend(
            lambda place: held_ref[place, rank],
            head,
            lists_ref,
            counts_ref,
            blocks,
        )


def temporal_kernel(
    heads, width, blocks, class_ref, lists_ref, counts_ref, packed_ref, out_ref
):
    half = heads // 2
    for rank in range(half):
        head = head_of_rank(class_ref, 1, rank, heads)

        def load(place):
            at = (place * half + rank) * width
            return packed_ref[:, at : at + width]

        out_ref[:, rank * width : (rank + 1) * width] = attend(
            load, head, lists_ref, counts_ref, blocks
        )


def place_heads(heads, width, class_ref, spatial_ref, temporal_ref, att_ref):
    rows = att_ref.shape[0] // 2
    side = lax.axis_index("head")
    for kind, ref in ((0, spatial_ref), (1, temporal_ref)):
        for rank in range(heads // 2):
            head = head_of_rank(class_ref, kind, rank, heads)
            for place, part in ((0, 1 - side), (1, side)):
                take = pl.ds(pl.multiple_of(part * rows, rows), rows)
                att_ref[place * rows : (place + 1) * rows, columns(head, width)] = ref[
                    take, rank * width : (rank + 1) * width
                ]


def project_pieces(attended, pieces, peer_ref, mine_ref):
    rows, cols = peer_ref.shape[0], pieces[0].shape[1]
    for index in range(0, len(pieces), 4):
        weight = jnp.concatenate(
            [
                jnp.concatenate([piece[...] for piece in pieces[at : at + 2]], axis=0)
                for at in range(index, index + 4, 2)
            ],
            axis=1,
        )
        total = jnp.dot(attended, weight, preferred_element_type=jnp.float32)
        total = total.astype(peer_ref.dtype)
        take = slice(index // 2 * cols, (index // 2 + 2) * cols)
        peer_ref[:, take] = total[:rows]
        mine_ref[:, take] = total[rows:]


def project_first_kernel(heads, width, class_ref, spatial_ref, temporal_ref, *refs):
    pieces, (peer_ref, mine_ref, attended_ref, att_ref) = refs[:-4], refs[-4:]
    place_heads(heads, width, class_ref, spatial_ref, temporal_ref, att_ref)
    depth = pieces[0].shape[0]
    half = lax.axis_index("groups")
    halves = (columns(half, depth), columns(1 - half, depth))
    for at, side in enumerate(halves):
        attended_ref[:, at * depth : (at + 1) * depth] = att_ref[:, side]
    project_pieces(attended_ref[...], pieces, peer_ref, mine_ref)


def project_last_kernel(attended_ref, *refs):
    pieces, (peer_ref, mine_ref) = refs[:-2], refs[-2:]
    project_pieces(attended_ref[...], pieces, peer_ref, mine_ref)


def project_whole_kernel(
    heads, width, class_ref, spatial_ref, temporal_ref, weight_ref, peer_ref, mine_ref, att_ref
):
    place_heads(heads, width, class_ref, spatial_ref, temporal_ref, att_ref)
    rows = peer_ref.shape[0]
    for place, out_ref in enumerate((peer_ref, mine_ref)):
        out_ref[...] = jnp.dot(
            att_ref[place * rows : (place + 1) * rows, :],
            weight_ref[...],
            preferred_element_type=jnp.float32,
        ).astype(out_ref.dtype)


def join_shards(shards, mine_ref, received_ref, out_ref, held_ref, sems):
    index = lax.axis_index("frame")
    line, pair = index // 2, lax.rem(index, 2)
    cols = mine_ref.shape[1] // len(shards)
    copies = []
    for at, (step, crossed) in enumerate(shards):
        source = lax.rem(line - step + 4, 4) * 2 + (1 - pair if crossed else pair)
        take = slice(at * cols, (at + 1) * cols)
        held_ref[:, take] = (
            mine_ref[:, take].astype(jnp.float32) + received_ref[:, take].astype(jnp.float32)
        ).astype(out_ref.dtype)
        copies.append(
            pltpu.make_async_copy(
                held_ref.at[:, take], out_ref.at[:, columns(source, cols)], sems.at[at]
            )
        )
        copies[-1].start()
    for copy in copies:
        copy.wait()


def join_first_kernel(shards, *refs):
    join_shards(shards, *refs)


def join_last_kernel(shards, mine_ref, received_ref, joined_ref, *refs):
    join_shards(shards, mine_ref, received_ref, *refs)


def swap_pair(piece):
    return lax.ppermute(piece, "frame", [(i, i ^ 1) for i in range(8)])


def swap_group(piece):
    return lax.ppermute(piece, "groups", [(0, 1), (1, 0)])


def next_line(piece):
    return lax.ppermute(piece, "frame", [(i, (i + 2) % 8) for i in range(8)])


def swap_side(portion):
    return lax.ppermute(portion, "head", [(0, 1), (1, 0)])


def tied(*values):
    return lax.optimization_barrier(values)


def on_device(
    head_queries, head_keys, head_values, out_weight, head_class, block_lists, block_counts
):
    pixels = head_queries.shape[0]
    heads = head_class.shape[0]
    half = heads // 2
    width = head_queries.shape[1] // heads
    blocks = block_counts.shape[2]
    frames = lax.axis_size("frame")
    groups = lax.axis_size("groups")
    model = out_weight.shape[1] * frames
    bf16 = functools.partial(jax.ShapeDtypeStruct, dtype=jnp.bfloat16)
    def call(kernel, ins, outs, *operands, scratch=(), out_spec=VMEM, aliases={}):
        return pl.pallas_call(
            kernel,
            out_shape=outs,
            in_specs=ins,
            out_specs=jax.tree.map(lambda _: out_spec, outs),
            input_output_aliases=aliases,
            scratch_shapes=scratch,
            compiler_params=PARAMS,
            cost_estimate=pl.CostEstimate(flops=next(v for k, v in COSTS.items() if k in str(kernel)) * 10**6, bytes_accessed=1000, transcendentals=0),
        )(*operands)

    def exchange(rows):
        split = rows.reshape(frames, pixels // frames, rows.shape[1])
        return lax.all_to_all(
            split, "frame", split_axis=0, concat_axis=0, tiled=True
        ).reshape(rows.shape)

    lists = (block_lists.reshape(heads, -1), block_counts.reshape(heads, -1))
    packed = call(
        functools.partial(pack_kernel, heads, width),
        [SMEM, ANY, ANY, ANY],
        bf16((pixels, 3 * half * width)),
        head_class,
        head_queries,
        head_keys,
        head_values,
        scratch=[pltpu.SemaphoreType.DMA((3, half))],
    )

    def spatial_heads():
        return call(
            functools.partial(spatial_kernel, heads, width, blocks),
            [SMEM, SMEM, SMEM, ANY, ANY, ANY],
            bf16((pixels, half * width)),
            head_class,
            *lists,
            head_queries,
            head_keys,
            head_values,
            scratch=[
                pltpu.VMEM((3, half, pixels, width), jnp.bfloat16),
                pltpu.SemaphoreType.DMA((3, half)),
            ],
        )

    def temporal_heads(arrived):
        return call(
            functools.partial(temporal_kernel, heads, width, blocks),
            [SMEM, SMEM, SMEM, VMEM],
            bf16((pixels, half * width)),
            head_class,
            *lists,
            arrived,
        )

    att_scratch = [pltpu.VMEM((pixels, heads * width), jnp.bfloat16)]
    if frames != 8 or groups != 2:
        spatial = spatial_heads()
        returned = exchange(temporal_heads(exchange(packed)))
        weight = lax.all_gather(out_weight, "frame", axis=1, tiled=True)
        peer, mine = call(
            functools.partial(project_whole_kernel, heads, width),
            [SMEM, VMEM, VMEM, VMEM],
            [bf16((pixels // 2, model))] * 2,
            head_class,
            spatial,
            returned,
            weight,
            scratch=att_scratch,
        )
        received = swap_side(peer)
        return (mine.astype(jnp.float32) + received.astype(jnp.float32)).astype(jnp.bfloat16)

    depth, cols = out_weight.shape[0] // 2, out_weight.shape[1]
    group = lax.axis_index("groups")
    own = lax.dynamic_slice_in_dim(out_weight, group * depth, depth, 0)
    rest = lax.dynamic_slice_in_dim(out_weight, (1 - group) * depth, depth, 0)

    def join(kernel, shards, mine, received, joined=None):
        return call(
            functools.partial(kernel, shards),
            [VMEM, VMEM] + ([] if joined is None else [HBM]),
            bf16((pixels // 2, model)),
            mine,
            received,
            *([] if joined is None else [joined]),
            scratch=[
                pltpu.VMEM(mine.shape, jnp.bfloat16),
                pltpu.SemaphoreType.DMA((len(shards),)),
            ],
            out_spec=HBM,
            aliases={} if joined is None else {2: 0},
        )

    arrived = exchange(packed)
    held_1, pair_0 = tied(next_line(own), swap_pair(own))
    pair_1, rest_1, pair_rest_0, spatial = tied(
        swap_pair(held_1), swap_group(held_1), swap_group(pair_0), spatial_heads()
    )
    pair_rest_1 = swap_group(pair_1)
    held_2 = next_line(held_1)
    returned = exchange(temporal_heads(arrived))
    held_3, pair_2, rest_2, pair_rest_1 = tied(
        next_line(held_2), swap_pair(held_2), swap_group(held_2), pair_rest_1
    )
    pair_3, rest_3, returned, pair_2 = tied(
        swap_pair(held_3), swap_group(held_3), returned, pair_2
    )
    pair_rest_2, pair_rest_3 = swap_group(pair_2), swap_pair(rest_3)
    pieces = [own, rest, pair_0, pair_rest_0, held_1, rest_1, pair_1, pair_rest_1]
    pieces += [held_2, rest_2, held_3, rest_3]
    peer, mine, attended = call(
        functools.partial(project_first_kernel, heads, width),
        [SMEM] + [VMEM] * (2 + len(pieces)),
        [bf16((pixels // 2, 6 * cols))] * 2 + [bf16((pixels, heads * width))],
        head_class,
        spatial,
        returned,
        *pieces,
        scratch=att_scratch,
    )
    received = swap_side(peer)
    last_peer, last_mine = call(
        project_last_kernel,
        [VMEM] * 5,
        [bf16((pixels // 2, 2 * cols))] * 2,
        attended,
        pair_2,
        pair_rest_2,
        pair_3,
        pair_rest_3,
    )
    last_received = swap_side(last_peer)
    joined = join(
        join_first_kernel, ((0, 0), (0, 1), (1, 0), (1, 1), (2, 0), (3, 0)), mine, received
    )
    return join(join_last_kernel, ((2, 1), (3, 1)), last_mine, last_received, joined)


def solution(mesh):
    placed = (
        P(("groups", "frame"), "head"),
        P(("groups", "frame"), "head"),
        P(("groups", "frame"), "head"),
        P("head", "frame"),
        P("head"),
        P("head", ("groups", "frame"), None, None),
        P("head", ("groups", "frame"), None),
    )
    return jax.shard_map(
        on_device,
        mesh=mesh,
        in_specs=placed,
        out_specs=P(("groups", "frame", "head"), None),
        check_vma=False,
    )
```
